128 devices in a mesh: section: 2 (over z_lo), dp: 16 (over y, x), tensor: 4 (over z_hi, core).
Axes of the slice: x: 4, y: 4, z: 4 (z_hi: 2, z_lo: 2; z = z_hi * 2 + z_lo), core: 2. Of those that a mesh axis runs over, the one named last changes fastest.
Arguments:
- images: bfloat16 [48, 577, 768], P('dp', None, 'tensor'), may hold values from -6 to 6
- slot_table: int32 [32], P('dp'), may hold values from 0 to 3, as said below
- ln1_gain: float32 [2, 768], P('section'), may hold values from 0.5 to 1.5
- ln1_bias: float32 [2, 768], P('section'), may hold values from -1.5 to 1.5
- qkv_weight: bfloat16 [2, 768, 3, 768], P('section', None, None, 'tensor'), may hold values from -0.21875 to 0.21875
- qv_bias: float32 [2, 2, 768], P('section', None, 'tensor'), may hold values from -1.5 to 1.5
- out_weight: bfloat16 [2, 768, 768], P('section', 'tensor'), may hold values from -0.875 to 0.875
- out_bias: float32 [2, 768], P('section'), may hold values from -1.5 to 1.5
- ln2_gain: float32 [2, 768], P('section'), may hold values from 0.5 to 1.5
- ln2_bias: float32 [2, 768], P('section'), may hold values from -1.5 to 1.5
- fc1_weight: bfloat16 [2, 768, 3072], P('section', None, 'tensor'), may hold values from -0.21875 to 0.21875
- fc1_bias: float32 [2, 3072], P('section', 'tensor'), may hold values from -1.5 to 1.5
- fc2_weight: bfloat16 [2, 3072, 768], P('section', 'tensor'), may hold values from -0.109375 to 0.109375
- fc2_bias: float32 [2, 768], P('section'), may hold values from -1.5 to 1.5
- cotangent: bfloat16 [48, 577, 768], P('dp', None, 'tensor'), may hold values from -6 to 6
Outputs:
- activations: bfloat16 [2, 48, 577, 768], P('section', 'dp', None, 'tensor')
- input_grads: float32 [2, 48, 577, 768], P('section', 'dp', None, 'tensor')
- ln1_gain_grad: float32 [2, 768], P('section', 'tensor')
- ln1_bias_grad: float32 [2, 768], P('section', 'tensor')
- qkv_weight_grad: float32 [2, 768, 3, 768], P('section', None, None, 'tensor')
- qv_bias_grad: float32 [2, 2, 768], P('section', None, 'tensor')
- out_weight_grad: float32 [2, 768, 768], P('section', 'tensor')
- out_bias_grad: float32 [2, 768], P('section', 'tensor')
- ln2_gain_grad: float32 [2, 768], P('section', 'tensor')
- ln2_bias_grad: float32 [2, 768], P('section', 'tensor')
- fc1_weight_grad: float32 [2, 768, 3072], P('section', None, 'tensor')
- fc1_bias_grad: float32 [2, 3072], P('section', 'tensor')
- fc2_weight_grad: float32 [2, 3072, 768], P('section', 'tensor')
- fc2_bias_grad: float32 [2, 768], P('section', 'tensor')
The draws below stay inside these ranges and needn't reach their ends.
Inputs may be any that keep to these rules, and one draw needn't show every extreme that they name: `slot_table`: within one data member's 2 entries, values below 3 are distinct; the value 3 means that the micro-batch has no image there.
All inputs are finite; a program needn't handle non-finite values.
Results may differ from the reference program's by a relative error of at most 0.0095.
Values may be sent and summed in bfloat16 or wider, within the bound.
No kernel may reach another device: no remote copies, remote signals or barrier semaphores. Data moves between devices by JAX's collectives and lax.ppermute only.
A program may use at most 192 MiB of HBM per device.

```python
import jax
import jax.numpy as jnp
from jax import lax

D = 768
HEADS = 12
HD = 64
FF = 3072
SEQ = 577
MICRO = 2
SLOTS = 3
IMAGES = 48
N_DP = 16


def draw_slot_table(key, part):
    first_key = jax.random.fold_in(key, 11)
    second_key = jax.random.fold_in(key, 12)
    third_key = jax.random.fold_in(key, 13)
    ranking = jax.random.randint(first_key, (N_DP, SLOTS), 0, 1 << 20) * SLOTS + jnp.arange(SLOTS, dtype=jnp.int32)[None, :]
    ordering = jnp.argsort(ranking, axis=1, stable=True).astype(jnp.int32)
    taken = ordering[:, :MICRO]
    emptied = jax.random.randint(second_key, (N_DP, MICRO), 0, 4) == 0
    forced = jax.random.randint(third_key, (), 0, N_DP)
    last_column = jnp.arange(MICRO) == MICRO - 1
    forced_rows = jnp.arange(N_DP)[:, None] == forced
    emptied = emptied | forced_rows & last_column[None, :]
    return jnp.where(emptied, SLOTS, taken).reshape(-1).astype(jnp.int32)


def block_scale(stream_key, extent, split, least, top_value):
    level = 1.0
    for dim, shards_of in split:
        heights = jax.random.uniform(jax.random.fold_in(jax.random.fold_in(stream_key, 6), dim), (shards_of,), jnp.float32, least / len(split), top_value / len(split))
        level = level * jnp.repeat(jnp.exp(heights), extent[dim] // shards_of).reshape((-1,) + (1,) * (len(extent) - 1 - dim))
    return level


def centred(key, extent, scale, reach, split=(), kind=jnp.bfloat16):
    values = jax.random.normal(key, extent, jnp.float32) * scale
    if len(split) > 0:
        values = block_scale(key, extent, split, -0.22, 0.18) * values
    return jnp.clip(values, min=-reach, max=reach).astype(kind)


def setup_inputs(seed: int = 0) -> dict:
    key_list = jax.random.split(jax.random.key(seed), 16)
    return {
        "images": centred(key_list[0], (IMAGES, SEQ, D), 1.0, 6.0, ((0, 16), (2, 4))),
        "slot_table": draw_slot_table(jax.random.fold_in(key_list[15], 71), 0),
        "ln1_gain": jnp.clip(1.0 + 0.1 * jax.random.normal(key_list[2], (2, D), jnp.float32), 0.5, 1.5),
        "ln1_bias": centred(key_list[3], (2, D), 0.3, 1.5, ((0, 2),), jnp.float32),
        "qkv_weight": centred(key_list[4], (2, D, 3, D), D ** -0.5, 0.21875, ((0, 2), (3, 4))),
        "qv_bias": centred(key_list[5], (2, 2, D), 0.3, 1.5, ((0, 2), (2, 4)), jnp.float32),
        "out_weight": centred(key_list[6], (2, D, D), (D // 16) ** -0.5, 0.875, ((0, 2), (1, 4))),
        "out_bias": centred(key_list[7], (2, D), 0.3, 1.5, ((0, 2),), jnp.float32),
        "ln2_gain": jnp.clip(1.0 + 0.1 * jax.random.normal(key_list[8], (2, D), jnp.float32), 0.5, 1.5),
        "ln2_bias": centred(key_list[9], (2, D), 0.3, 1.5, ((0, 2),), jnp.float32),
        "fc1_weight": centred(key_list[10], (2, D, FF), D ** -0.5, 0.21875, ((0, 2), (2, 4))),
        "fc1_bias": centred(key_list[11], (2, FF), 0.3, 1.5, ((0, 2), (1, 4)), jnp.float32),
        "fc2_weight": centred(key_list[12], (2, FF, D), FF ** -0.5, 0.109375, ((0, 2), (1, 4))),
        "fc2_bias": centred(key_list[13], (2, D), 0.3, 1.5, ((0, 2),), jnp.float32),
        "cotangent": centred(key_list[14], (IMAGES, SEQ, D), 1.0, 6.0, ((0, 16), (2, 4))),
    }


epsilon = 1e-06
highest = lax.Precision.HIGHEST

@jax.custom_vjp
def low(v):
    return lax.optimization_barrier(v.astype(jnp.bfloat16)).astype(jnp.float32)

@jax.custom_vjp
def low_back(v):
    return v

def low_keep(v):
    return (low(v), None)

def low_pass(kept, grad):
    return (grad,)

def back_keep(v):
    return (v, None)

def back_low(kept, grad):
    return (low(grad),)
low.defvjp(low_keep, low_pass)
low_back.defvjp(back_keep, back_low)

def normalize(values, gain, shift):
    center = values - lax.optimization_barrier(jnp.mean(values, axis=-1, keepdims=True))
    spread = lax.optimization_barrier(jnp.mean(center * center, axis=-1, keepdims=True))
    return center * lax.rsqrt(spread + epsilon) * gain + shift

def encoder_layer(stream, params):
    first_norm_gain, first_norm_bias, qkv_mat, qv_add, out_mat, out_add, second_norm_gain, second_norm_bias, up_mat, up_add, down_mat, down_add = params
    normed = low(normalize(stream, first_norm_gain, first_norm_bias))
    project = jnp.dot(normed, qkv_mat.reshape(D, 3 * D), precision=highest).reshape(SEQ, 3, D)
    queries = low(low_back(project[:, 0] + qv_add[0])).reshape(SEQ, HEADS, HD)
    keys_all = low(low_back(project[:, 1])).reshape(SEQ, HEADS, HD)
    values_all = low(low_back(project[:, 2] + qv_add[1])).reshape(SEQ, HEADS, HD)
    scores = low_back(jnp.einsum('qhd,khd->hqk', queries, keys_all, precision=highest) * HD ** (-0.5))
    weights = low(jax.nn.softmax(scores, axis=-1))
    attended = low(low_back(jnp.einsum('hqk,khd->qhd', weights, values_all, precision=highest).reshape(SEQ, D)))
    middle = stream + low_back(jnp.dot(attended, out_mat, precision=highest)) + out_add
    second_normalized = low(normalize(low(middle), second_norm_gain, second_norm_bias))
    hidden_pre = low_back(jnp.dot(second_normalized, up_mat, precision=highest) + up_add)
    hidden = low(jax.nn.gelu(hidden_pre, approximate=False))
    return middle + low_back(jnp.dot(hidden, down_mat, precision=highest)) + down_add

def reference(images, slot_table, ln1_gain, ln1_bias, qkv_weight, qv_bias, out_weight, out_bias, ln2_gain, ln2_bias, fc1_weight, fc1_bias, fc2_weight, fc2_bias, cotangent):
    params = [weight_arg.astype(jnp.float32) for weight_arg in (ln1_gain, ln1_bias, qkv_weight, qv_bias, out_weight, out_bias, ln2_gain, ln2_bias, fc1_weight, fc1_bias, fc2_weight, fc2_bias)]
    section_one = tuple((weight_arg[0] for weight_arg in params))
    section_two = tuple((weight_arg[1] for weight_arg in params))
    slot_rows = slot_table.reshape(N_DP, MICRO)
    assigned = jnp.any(slot_rows[:, :, None] == jnp.arange(SLOTS, dtype=jnp.int32)[None, None, :], axis=1)
    live_mask = assigned.reshape(N_DP * SLOTS, 1, 1).astype(jnp.float32)
    inputs = images.astype(jnp.float32)
    offsets = jnp.zeros_like(inputs)

    def forward(inputs, offsets, section_one, section_two):

        def one_image(image_pair):
            tokens_in, offset = image_pair
            out_first = encoder_layer(tokens_in, section_one)
            out_second = encoder_layer(low(low_back(out_first) + offset), section_two)
            return (out_first, out_second)
        return lax.map(jax.checkpoint(one_image), (inputs, offsets))
    (out_first, out_second), pullback = jax.vjp(forward, inputs, offsets, section_one, section_two)
    grad_input, grad_middle, grads_one, grads_two = pullback((jnp.zeros_like(out_first), cotangent.astype(jnp.float32) * live_mask))
    activations = (jnp.stack([out_first, out_second]) * live_mask[None]).astype(jnp.bfloat16)
    input_grads = jnp.stack([grad_input, grad_middle]) * live_mask[None]
    stacked = [jnp.stack([grads_one[number], grads_two[number]]) for number in range(12)]
    return (activations, input_grads, stacked[0], stacked[1], stacked[2], stacked[3], stacked[4], stacked[5], stacked[6], stacked[7], stacked[8], stacked[9], stacked[10], stacked[11])
```

```python
from functools import partial

import jax
import jax.numpy as jnp
from jax import lax
from jax.sharding import PartitionSpec as P

HD = 64


epsilon = 1e-06


def shifted(block, axis, distance):
    devices = range(lax.axis_size(axis))
    route = [(i - distance, i) for i in devices if i - distance in devices]
    return lax.ppermute(block, axis, route)


def standardize_rows(values):
    row_means = jnp.mean(values, axis=1, keepdims=True)
    center = values - row_means
    inverse = lax.rsqrt(jnp.mean(center * center, axis=1, keepdims=True) + epsilon)
    return (center * inverse, row_means, inverse)


def contract_rows(left_side, right_side):
    return lax.dot_general(
        left_side, right_side, (((0,), (0,)), ((), ())), preferred_element_type=jnp.float32
    )


def contract_cols(left_side, right_side):
    return lax.dot_general(
        left_side, right_side, (((1,), (1,)), ((), ())), preferred_element_type=jnp.float32
    )


def member_sum(gradients):
    return lax.psum(gradients, "dp")


def tensor_sum(partial_value):
    return lax.psum(partial_value.astype(jnp.bfloat16), "tensor").astype(jnp.float32)


def layer_forward(partial_residual, params, column):
    (
        first_norm_gain,
        first_norm_bias,
        qkv_mat,
        qv_add,
        out_mat,
        out_add,
        second_norm_gain,
        second_norm_bias,
        up_mat,
        up_add,
        down_mat,
        down_add,
    ) = params
    rows_count = partial_residual.shape[0]
    part_width = partial_residual.shape[1]
    hidden_width = first_norm_gain.shape[0]
    head_count = part_width // HD

    complete_residual = lax.all_gather(partial_residual, "tensor", axis=1, tiled=True).astype(
        jnp.float32
    )
    first_centered_unit, first_row_averages, first_inverse_deviation = standardize_rows(
        complete_residual
    )
    first_normalized = (first_centered_unit * first_norm_gain + first_norm_bias).astype(
        jnp.bfloat16
    )
    projected = jnp.dot(
        first_normalized,
        qkv_mat.reshape(hidden_width, 3 * part_width),
        preferred_element_type=jnp.float32,
    ).reshape(rows_count, 3, part_width)
    queries = (projected[:, 0] + qv_add[0]).astype(jnp.bfloat16).reshape(rows_count, head_count, HD)
    keys_part = projected[:, 1].astype(jnp.bfloat16).reshape(rows_count, head_count, HD)
    values_part = (
        (projected[:, 2] + qv_add[1]).astype(jnp.bfloat16).reshape(rows_count, head_count, HD)
    )
    scores = jnp.einsum(
        "qhd,khd->hqk", queries, keys_part, preferred_element_type=jnp.float32
    ) * HD ** (-0.5)
    totals = jax.nn.logsumexp(scores, axis=2, keepdims=True)
    probabilities = jnp.exp(scores - totals)
    attended = (
        jnp.einsum(
            "hqk,khd->qhd",
            probabilities.astype(jnp.bfloat16),
            values_part,
            preferred_element_type=jnp.float32,
        )
        .reshape(rows_count, part_width)
        .astype(jnp.bfloat16)
    )
    branch = tensor_sum(jnp.dot(attended, out_mat, preferred_element_type=jnp.float32))
    middle = complete_residual + branch + out_add
    middle_rounded = middle.astype(jnp.bfloat16).astype(jnp.float32)
    second_centered_unit, second_row_averages, second_inverse_deviation = standardize_rows(
        middle_rounded
    )
    second_normalized = (second_centered_unit * second_norm_gain + second_norm_bias).astype(
        jnp.bfloat16
    )
    hidden_pre = jnp.dot(second_normalized, up_mat, preferred_element_type=jnp.float32) + up_add
    hidden = jax.nn.gelu(hidden_pre, approximate=False).astype(jnp.bfloat16)
    feed_out = tensor_sum(jnp.dot(hidden, down_mat, preferred_element_type=jnp.float32))
    result = middle + feed_out + down_add
    result_part = lax.dynamic_slice_in_dim(result, column, part_width, 1)
    saved_state = (
        first_centered_unit,
        first_inverse_deviation,
        first_normalized,
        queries,
        keys_part,
        values_part,
        totals,
        attended,
        second_centered_unit,
        second_inverse_deviation,
        second_normalized,
        hidden_pre,
        hidden,
    )
    return (result_part.astype(jnp.bfloat16), saved_state)


def layer_backward(grad_part, saved_state, params, column, grad_sums):
    (
        first_norm_gain,
        first_norm_bias,
        qkv_mat,
        qv_add,
        out_mat,
        out_add,
        second_norm_gain,
        second_norm_bias,
        up_mat,
        up_add,
        down_mat,
        down_add,
    ) = params
    (
        first_centered_unit,
        first_inverse_deviation,
        first_normalized,
        queries,
        keys_part,
        values_part,
        totals,
        attended,
        second_centered_unit,
        second_inverse_deviation,
        second_normalized,
        hidden_pre,
        hidden,
    ) = saved_state
    rows_count = grad_part.shape[0]
    part_width = grad_part.shape[1]
    hidden_width = first_norm_gain.shape[0]
    head_count = part_width // HD

    def local_cols(matrix):
        return lax.dynamic_slice_in_dim(matrix, column, part_width, 1)

    grad_full_bf16 = lax.all_gather(grad_part, "tensor", axis=1, tiled=True)
    grad_full = grad_full_bf16.astype(jnp.float32)
    down_grad = contract_rows(hidden, grad_full_bf16)
    down_add_grad = jnp.sum(local_cols(grad_full), axis=0)
    hidden_grad = contract_cols(grad_full_bf16, down_mat)
    unused_value, gelu_back = jax.vjp(partial(jax.nn.gelu, approximate=False), hidden_pre)
    pre_grad = gelu_back(hidden_grad)[0].astype(jnp.bfloat16)
    up_grad = contract_rows(second_normalized, pre_grad)
    up_add_grad = jnp.sum(pre_grad.astype(jnp.float32), axis=0)
    normalized_gradient = tensor_sum(contract_cols(pre_grad, up_mat))
    second_gain_gradient = jnp.sum(local_cols(normalized_gradient * second_centered_unit), axis=0)
    bias_two_grad = jnp.sum(local_cols(normalized_gradient), axis=0)
    second_rescaled = normalized_gradient * second_norm_gain
    first_running_total = jnp.sum(second_rescaled, axis=1, keepdims=True)
    second_running_total = jnp.sum(second_rescaled * second_centered_unit, axis=1, keepdims=True)
    middle_grad = grad_full + second_inverse_deviation * (
        second_rescaled
        - first_running_total / hidden_width
        - second_centered_unit * second_running_total / hidden_width
    )
    feed_grads = (
        second_gain_gradient,
        bias_two_grad,
        up_grad,
        up_add_grad,
        down_grad,
        down_add_grad,
    )
    feed_grads = tuple((older + newer for older, newer in zip(grad_sums[6:], feed_grads)))
    branch_grad = middle_grad.astype(jnp.bfloat16)
    out_grad = contract_rows(attended, branch_grad)
    out_add_grad = jnp.sum(local_cols(middle_grad), axis=0)
    attended_grad = (
        contract_cols(branch_grad, out_mat).astype(jnp.bfloat16).reshape(rows_count, head_count, HD)
    )
    scale_factor = HD ** (-0.5)
    scores = (
        jnp.einsum("qhd,khd->hqk", queries, keys_part, preferred_element_type=jnp.float32)
        * scale_factor
    )
    probabilities = jnp.exp(scores - totals)
    values_grad = jnp.einsum(
        "hqk,qhd->khd",
        probabilities.astype(jnp.bfloat16),
        attended_grad,
        preferred_element_type=jnp.float32,
    )
    weight_grad = jnp.einsum(
        "qhd,khd->hqk", attended_grad, values_part, preferred_element_type=jnp.float32
    )
    rowdot = jnp.sum(probabilities * weight_grad, axis=2, keepdims=True)
    score_grad = (probabilities * (weight_grad - rowdot)).astype(jnp.bfloat16)
    query_grad = (
        jnp.einsum("hqk,khd->qhd", score_grad, keys_part, preferred_element_type=jnp.float32)
        * scale_factor
    )
    key_grad = (
        jnp.einsum("hqk,qhd->khd", score_grad, queries, preferred_element_type=jnp.float32)
        * scale_factor
    )
    projected_grad = jnp.stack(
        [
            query_grad.reshape(rows_count, part_width),
            key_grad.reshape(rows_count, part_width),
            values_grad.reshape(rows_count, part_width),
        ],
        axis=1,
    ).astype(jnp.bfloat16)
    flat_grad = projected_grad.reshape(rows_count, 3 * part_width)
    qkv_grad = contract_rows(first_normalized, flat_grad).reshape(hidden_width, 3, part_width)
    qv_add_grad = jnp.stack(
        [
            jnp.sum(projected_grad[:, 0].astype(jnp.float32), axis=0),
            jnp.sum(projected_grad[:, 2].astype(jnp.float32), axis=0),
        ]
    )
    first_normalized_gradient = tensor_sum(
        contract_cols(flat_grad, qkv_mat.reshape(hidden_width, 3 * part_width))
    )
    first_gain_gradient = jnp.sum(
        local_cols(first_normalized_gradient * first_centered_unit), axis=0
    )
    bias_one_grad = jnp.sum(local_cols(first_normalized_gradient), axis=0)
    first_rescaled = first_normalized_gradient * first_norm_gain
    third_running_total = jnp.sum(first_rescaled, axis=1, keepdims=True)
    fourth_running_total = jnp.sum(first_rescaled * first_centered_unit, axis=1, keepdims=True)
    stream_grad = middle_grad + first_inverse_deviation * (
        first_rescaled
        - third_running_total / hidden_width
        - first_centered_unit * fourth_running_total / hidden_width
    )
    attention_grads = (
        first_gain_gradient,
        bias_one_grad,
        qkv_grad,
        qv_add_grad,
        out_grad,
        out_add_grad,
    )
    attention_grads = tuple((older + newer for older, newer in zip(grad_sums[:6], attention_grads)))
    return (local_cols(stream_grad), attention_grads + feed_grads)


def shards(
    images,
    slot_table,
    ln1_gain,
    ln1_bias,
    qkv_weight,
    qv_bias,
    out_weight,
    out_bias,
    ln2_gain,
    ln2_bias,
    fc1_weight,
    fc1_bias,
    fc2_weight,
    fc2_bias,
    cotangent,
):
    params = tuple(
        (
            weight_arg[0]
            for weight_arg in (
                ln1_gain,
                ln1_bias,
                qkv_weight,
                qv_bias,
                out_weight,
                out_bias,
                ln2_gain,
                ln2_bias,
                fc1_weight,
                fc1_bias,
                fc2_weight,
                fc2_bias,
            )
        )
    )
    section_index = lax.axis_index("section")
    part_width = images.shape[2]
    column = lax.axis_index("tensor") * part_width
    slot_count = images.shape[0]
    micro_count = slot_table.shape[0]
    slot_ids = jnp.arange(slot_count, dtype=jnp.int32)

    def locate(batch_index):
        clipped = jnp.clip(batch_index, 0, micro_count - 1)
        chosen = lax.dynamic_index_in_dim(slot_table, clipped, 0, keepdims=False)
        active = (batch_index >= 0) & (batch_index < micro_count) & (chosen < slot_count)
        return (jnp.minimum(chosen, slot_count - 1), active, (slot_ids == chosen) & active)

    received = jnp.zeros(images.shape[1:], jnp.bfloat16)
    layer_outputs = jnp.zeros(images.shape, jnp.bfloat16)
    saved_states = []
    for step_index in range(micro_count + 1):
        where_from, active, placed = locate(step_index - section_index)
        own_image = lax.dynamic_index_in_dim(images, where_from, 0, keepdims=False)
        entering = jnp.where(section_index == 0, own_image, received)
        leaving, layer_state = layer_forward(entering, params, column)
        saved_states.append(layer_state)
        layer_outputs = layer_outputs + placed[:, None, None].astype(jnp.bfloat16) * leaving[None]
        if step_index < micro_count:
            received = shifted(leaving, "section", 1)

    def zeros_of(extent):
        return jnp.zeros(extent, jnp.float32)

    grad_sums = (
        zeros_of((part_width,)),
        zeros_of((part_width,)),
        zeros_of(params[2].shape),
        zeros_of(params[3].shape),
        zeros_of(params[4].shape),
        zeros_of((part_width,)),
        zeros_of((part_width,)),
        zeros_of((part_width,)),
        zeros_of(params[8].shape),
        zeros_of(params[9].shape),
        zeros_of(params[10].shape),
        zeros_of((part_width,)),
    )
    coming_back = jnp.zeros(images.shape[1:], jnp.bfloat16)
    grads_in = jnp.zeros(images.shape, jnp.float32)
    for step_index in range(micro_count + 1):
        where_from, active, placed = locate(micro_count - step_index - section_index)
        own_grad = lax.dynamic_index_in_dim(cotangent, where_from, 0, keepdims=False)
        entering = jnp.where(
            active, jnp.where(section_index == 1, own_grad, coming_back), jnp.zeros_like(own_grad)
        )
        stream_grad, grad_sums = layer_backward(
            entering, saved_states[micro_count - step_index], params, column, grad_sums
        )
        grads_in = grads_in + placed[:, None, None].astype(jnp.float32) * stream_grad[None]
        if step_index < micro_count:
            coming_back = shifted(stream_grad.astype(jnp.bfloat16), "section", -1)
    grad_sums = member_sum(grad_sums)
    return (layer_outputs[None], grads_in[None]) + tuple((gradient[None] for gradient in grad_sums))


def solution(mesh):
    in_specs = (
        P("dp", None, "tensor"),
        P("dp"),
        P("section", None),
        P("section", None),
        P("section", None, None, "tensor"),
        P("section", None, "tensor"),
        P("section", "tensor", None),
        P("section", None),
        P("section", None),
        P("section", None),
        P("section", None, "tensor"),
        P("section", "tensor"),
        P("section", "tensor", None),
        P("section", None),
        P("dp", None, "tensor"),
    )
    out_specs = (
        P("section", "dp", None, "tensor"),
        P("section", "dp", None, "tensor"),
        P("section", "tensor"),
        P("section", "tensor"),
        P("section", None, None, "tensor"),
        P("section", None, "tensor"),
        P("section", "tensor", None),
        P("section", "tensor"),
        P("section", "tensor"),
        P("section", "tensor"),
        P("section", None, "tensor"),
        P("section", "tensor"),
        P("section", "tensor", None),
        P("section", "tensor"),
    )
    return jax.shard_map(shards, mesh=mesh, in_specs=in_specs, out_specs=out_specs, check_vma=False)
```

```python
from functools import partial

import jax
import jax.numpy as jnp
from jax import lax
from jax.sharding import PartitionSpec as P

HD = 64


epsilon = 1e-06


def shifted(block, axis, distance):
    devices = range(lax.axis_size(axis))
    route = [(i - distance, i) for i in devices if i - distance in devices]
    return lax.ppermute(block, axis, route)


def standardize_rows(values):
    row_means = jnp.mean(values, axis=1, keepdims=True)
    center = values - row_means
    inverse = lax.rsqrt(jnp.mean(center * center, axis=1, keepdims=True) + epsilon)
    return (center * inverse, row_means, inverse)


def contract_rows(left_side, right_side):
    return lax.dot_general(
        left_side, right_side, (((0,), (0,)), ((), ())), preferred_element_type=jnp.float32
    )


def contract_cols(left_side, right_side):
    return lax.dot_general(
        left_side, right_side, (((1,), (1,)), ((), ())), preferred_element_type=jnp.float32
    )


def member_sum(gradients):
    return lax.psum(gradients, "dp")


def tensor_scatter_sum(partial_value):
    group = lax.axis_size("tensor")
    rows_count, full_width = partial_value.shape
    pieces = lax.all_to_all(
        partial_value.astype(jnp.bfloat16), "tensor", 1, 0, tiled=True
    ).reshape(group, rows_count, full_width // group)
    return jnp.sum(pieces.astype(jnp.float32), axis=0)


def tensor_sum(partial_value):
    summed = tensor_scatter_sum(partial_value)
    return lax.all_gather(summed.astype(jnp.bfloat16), "tensor", axis=1, tiled=True).astype(
        jnp.float32
    )


def layer_forward(partial_residual, params, column):
    (
        first_norm_gain,
        first_norm_bias,
        qkv_mat,
        qv_add,
        out_mat,
        out_add,
        second_norm_gain,
        second_norm_bias,
        up_mat,
        up_add,
        down_mat,
        down_add,
    ) = params
    rows_count = partial_residual.shape[0]
    part_width = partial_residual.shape[1]
    hidden_width = first_norm_gain.shape[0]
    head_count = part_width // HD

    complete_residual = lax.all_gather(partial_residual, "tensor", axis=1, tiled=True).astype(
        jnp.float32
    )
    first_centered_unit, first_row_averages, first_inverse_deviation = standardize_rows(
        complete_residual
    )
    first_normalized = (first_centered_unit * first_norm_gain + first_norm_bias).astype(
        jnp.bfloat16
    )
    projected = jnp.dot(
        first_normalized,
        qkv_mat.reshape(hidden_width, 3 * part_width),
        preferred_element_type=jnp.float32,
    ).reshape(rows_count, 3, part_width)
    queries = (projected[:, 0] + qv_add[0]).astype(jnp.bfloat16).reshape(rows_count, head_count, HD)
    keys_part = projected[:, 1].astype(jnp.bfloat16).reshape(rows_count, head_count, HD)
    values_part = (
        (projected[:, 2] + qv_add[1]).astype(jnp.bfloat16).reshape(rows_count, head_count, HD)
    )
    scores = jnp.einsum(
        "qhd,khd->hqk", queries, keys_part, preferred_element_type=jnp.float32
    ) * HD ** (-0.5)
    totals = jax.nn.logsumexp(scores, axis=2, keepdims=True)
    probabilities = jnp.exp(scores - totals)
    attended = (
        jnp.einsum(
            "hqk,khd->qhd",
            probabilities.astype(jnp.bfloat16),
            values_part,
            preferred_element_type=jnp.float32,
        )
        .reshape(rows_count, part_width)
        .astype(jnp.bfloat16)
    )
    branch = tensor_sum(jnp.dot(attended, out_mat, preferred_element_type=jnp.float32))
    middle = complete_residual + branch + out_add
    middle_rounded = middle.astype(jnp.bfloat16).astype(jnp.float32)
    second_centered_unit, second_row_averages, second_inverse_deviation = standardize_rows(
        middle_rounded
    )
    second_normalized = (second_centered_unit * second_norm_gain + second_norm_bias).astype(
        jnp.bfloat16
    )
    hidden_pre = jnp.dot(second_normalized, up_mat, preferred_element_type=jnp.float32) + up_add
    hidden = jax.nn.gelu(hidden_pre, approximate=False).astype(jnp.bfloat16)
    feed_out = tensor_scatter_sum(jnp.dot(hidden, down_mat, preferred_element_type=jnp.float32))
    result_part = (
        lax.dynamic_slice_in_dim(middle, column, part_width, 1)
        + feed_out
        + lax.dynamic_slice_in_dim(down_add, column, part_width, 0)
    )
    saved_state = (
        first_centered_unit,
        first_inverse_deviation,
        first_normalized,
        queries,
        keys_part,
        values_part,
        totals,
        attended,
        second_centered_unit,
        second_inverse_deviation,
        second_normalized,
        hidden_pre,
        hidden,
    )
    return (result_part.astype(jnp.bfloat16), saved_state)


def layer_backward(grad_part, saved_state, params, column, grad_sums):
    (
        first_norm_gain,
        first_norm_bias,
        qkv_mat,
        qv_add,
        out_mat,
        out_add,
        second_norm_gain,
        second_norm_bias,
        up_mat,
        up_add,
        down_mat,
        down_add,
    ) = params
    (
        first_centered_unit,
        first_inverse_deviation,
        first_normalized,
        queries,
        keys_part,
        values_part,
        totals,
        attended,
        second_centered_unit,
        second_inverse_deviation,
        second_normalized,
        hidden_pre,
        hidden,
    ) = saved_state
    rows_count = grad_part.shape[0]
    part_width = grad_part.shape[1]
    hidden_width = first_norm_gain.shape[0]
    head_count = part_width // HD

    def local_cols(matrix):
        return lax.dynamic_slice_in_dim(matrix, column, part_width, 1)

    grad_full_bf16 = lax.all_gather(grad_part, "tensor", axis=1, tiled=True)
    grad_full = grad_full_bf16.astype(jnp.float32)
    down_grad = contract_rows(hidden, grad_full_bf16)
    down_add_grad = jnp.sum(local_cols(grad_full), axis=0)
    hidden_grad = contract_cols(grad_full_bf16, down_mat)
    unused_value, gelu_back = jax.vjp(partial(jax.nn.gelu, approximate=False), hidden_pre)
    pre_grad = gelu_back(hidden_grad)[0].astype(jnp.bfloat16)
    up_grad = contract_rows(second_normalized, pre_grad)
    up_add_grad = jnp.sum(pre_grad.astype(jnp.float32), axis=0)
    normalized_gradient = tensor_sum(contract_cols(pre_grad, up_mat))
    second_gain_gradient = jnp.sum(local_cols(normalized_gradient * second_centered_unit), axis=0)
    bias_two_grad = jnp.sum(local_cols(normalized_gradient), axis=0)
    second_rescaled = normalized_gradient * second_norm_gain
    first_running_total = jnp.sum(second_rescaled, axis=1, keepdims=True)
    second_running_total = jnp.sum(second_rescaled * second_centered_unit, axis=1, keepdims=True)
    middle_grad = grad_full + second_inverse_deviation * (
        second_rescaled
        - first_running_total / hidden_width
        - second_centered_unit * second_running_total / hidden_width
    )
    feed_grads = (
        second_gain_gradient,
        bias_two_grad,
        up_grad,
        up_add_grad,
        down_grad,
        down_add_grad,
    )
    feed_grads = tuple((older + newer for older, newer in zip(grad_sums[6:], feed_grads)))
    branch_grad = middle_grad.astype(jnp.bfloat16)
    out_grad = contract_rows(attended, branch_grad)
    out_add_grad = jnp.sum(local_cols(middle_grad), axis=0)
    attended_grad = (
        contract_cols(branch_grad, out_mat).astype(jnp.bfloat16).reshape(rows_count, head_count, HD)
    )
    scale_factor = HD ** (-0.5)
    scores = (
        jnp.einsum("qhd,khd->hqk", queries, keys_part, preferred_element_type=jnp.float32)
        * scale_factor
    )
    probabilities = jnp.exp(scores - totals)
    values_grad = jnp.einsum(
        "hqk,qhd->khd",
        probabilities.astype(jnp.bfloat16),
        attended_grad,
        preferred_element_type=jnp.float32,
    )
    weight_grad = jnp.einsum(
        "qhd,khd->hqk", attended_grad, values_part, preferred_element_type=jnp.float32
    )
    rowdot = jnp.sum(probabilities * weight_grad, axis=2, keepdims=True)
    score_grad = (probabilities * (weight_grad - rowdot)).astype(jnp.bfloat16)
    query_grad = (
        jnp.einsum("hqk,khd->qhd", score_grad, keys_part, preferred_element_type=jnp.float32)
        * scale_factor
    )
    key_grad = (
        jnp.einsum("hqk,qhd->khd", score_grad, queries, preferred_element_type=jnp.float32)
        * scale_factor
    )
    projected_grad = jnp.stack(
        [
            query_grad.reshape(rows_count, part_width),
            key_grad.reshape(rows_count, part_width),
            values_grad.reshape(rows_count, part_width),
        ],
        axis=1,
    ).astype(jnp.bfloat16)
    flat_grad = projected_grad.reshape(rows_count, 3 * part_width)
    qkv_grad = contract_rows(first_normalized, flat_grad).reshape(hidden_width, 3, part_width)
    qv_add_grad = jnp.stack(
        [
            jnp.sum(projected_grad[:, 0].astype(jnp.float32), axis=0),
            jnp.sum(projected_grad[:, 2].astype(jnp.float32), axis=0),
        ]
    )
    first_normalized_gradient = tensor_sum(
        contract_cols(flat_grad, qkv_mat.reshape(hidden_width, 3 * part_width))
    )
    first_gain_gradient = jnp.sum(
        local_cols(first_normalized_gradient * first_centered_unit), axis=0
    )
    bias_one_grad = jnp.sum(local_cols(first_normalized_gradient), axis=0)
    first_rescaled = first_normalized_gradient * first_norm_gain
    third_running_total = jnp.sum(first_rescaled, axis=1, keepdims=True)
    fourth_running_total = jnp.sum(first_rescaled * first_centered_unit, axis=1, keepdims=True)
    stream_grad = middle_grad + first_inverse_deviation * (
        first_rescaled
        - third_running_total / hidden_width
        - first_centered_unit * fourth_running_total / hidden_width
    )
    attention_grads = (
        first_gain_gradient,
        bias_one_grad,
        qkv_grad,
        qv_add_grad,
        out_grad,
        out_add_grad,
    )
    attention_grads = tuple((older + newer for older, newer in zip(grad_sums[:6], attention_grads)))
    return (local_cols(stream_grad), attention_grads + feed_grads)


def shards(
    images,
    slot_table,
    ln1_gain,
    ln1_bias,
    qkv_weight,
    qv_bias,
    out_weight,
    out_bias,
    ln2_gain,
    ln2_bias,
    fc1_weight,
    fc1_bias,
    fc2_weight,
    fc2_bias,
    cotangent,
):
    params = tuple(
        (
            weight_arg[0]
            for weight_arg in (
                ln1_gain,
                ln1_bias,
                qkv_weight,
                qv_bias,
                out_weight,
                out_bias,
                ln2_gain,
                ln2_bias,
                fc1_weight,
                fc1_bias,
                fc2_weight,
                fc2_bias,
            )
        )
    )
    section_index = lax.axis_index("section")
    part_width = images.shape[2]
    column = lax.axis_index("tensor") * part_width
    slot_count = images.shape[0]
    micro_count = slot_table.shape[0]
    slot_ids = jnp.arange(slot_count, dtype=jnp.int32)

    def locate(batch_index):
        clipped = jnp.clip(batch_index, 0, micro_count - 1)
        chosen = lax.dynamic_index_in_dim(slot_table, clipped, 0, keepdims=False)
        active = (batch_index >= 0) & (batch_index < micro_count) & (chosen < slot_count)
        return (jnp.minimum(chosen, slot_count - 1), active, (slot_ids == chosen) & active)

    received = jnp.zeros(images.shape[1:], jnp.bfloat16)
    layer_outputs = jnp.zeros(images.shape, jnp.bfloat16)
    saved_states = []
    for step_index in range(micro_count + 1):
        where_from, active, placed = locate(step_index - section_index)
        own_image = lax.dynamic_index_in_dim(images, where_from, 0, keepdims=False)
        entering = jnp.where(section_index == 0, own_image, received)
        leaving, layer_state = layer_forward(entering, params, column)
        saved_states.append(layer_state)
        layer_outputs = layer_outputs + placed[:, None, None].astype(jnp.bfloat16) * leaving[None]
        if step_index < micro_count:
            received = shifted(leaving, "section", 1)

    def zeros_of(extent):
        return jnp.zeros(extent, jnp.float32)

    grad_sums = (
        zeros_of((part_width,)),
        zeros_of((part_width,)),
        zeros_of(params[2].shape),
        zeros_of(params[3].shape),
        zeros_of(params[4].shape),
        zeros_of((part_width,)),
        zeros_of((part_width,)),
        zeros_of((part_width,)),
        zeros_of(params[8].shape),
        zeros_of(params[9].shape),
        zeros_of(params[10].shape),
        zeros_of((part_width,)),
    )
    coming_back = jnp.zeros(images.shape[1:], jnp.bfloat16)
    grads_in = jnp.zeros(images.shape, jnp.float32)
    for step_index in range(micro_count + 1):
        where_from, active, placed = locate(micro_count - step_index - section_index)
        own_grad = lax.dynamic_index_in_dim(cotangent, where_from, 0, keepdims=False)
        entering = jnp.where(
            active, jnp.where(section_index == 1, own_grad, coming_back), jnp.zeros_like(own_grad)
        )
        stream_grad, grad_sums = layer_backward(
            entering, saved_states[micro_count - step_index], params, column, grad_sums
        )
        grads_in = grads_in + placed[:, None, None].astype(jnp.float32) * stream_grad[None]
        if step_index < micro_count:
            coming_back = shifted(stream_grad.astype(jnp.bfloat16), "section", -1)
    flat_sums = member_sum(jnp.concatenate([gradient.reshape(-1) for gradient in grad_sums]))
    unpacked = []
    offset = 0
    for gradient in grad_sums:
        unpacked.append(flat_sums[offset : offset + gradient.size].reshape(gradient.shape))
        offset += gradient.size
    grad_sums = tuple(unpacked)
    return (layer_outputs[None], grads_in[None]) + tuple((gradient[None] for gradient in grad_sums))


def solution(mesh):
    in_specs = (
        P("dp", None, "tensor"),
        P("dp"),
        P("section", None),
        P("section", None),
        P("section", None, None, "tensor"),
        P("section", None, "tensor"),
        P("section", "tensor", None),
        P("section", None),
        P("section", None),
        P("section", None),
        P("section", None, "tensor"),
        P("section", "tensor"),
        P("section", "tensor", None),
        P("section", None),
        P("dp", None, "tensor"),
    )
    out_specs = (
        P("section", "dp", None, "tensor"),
        P("section", "dp", None, "tensor"),
        P("section", "tensor"),
        P("section", "tensor"),
        P("section", None, None, "tensor"),
        P("section", None, "tensor"),
        P("section", "tensor", None),
        P("section", "tensor"),
        P("section", "tensor"),
        P("section", "tensor"),
        P("section", None, "tensor"),
        P("section", "tensor"),
        P("section", "tensor", None),
        P("section", "tensor"),
    )
    return jax.shard_map(shards, mesh=mesh, in_specs=in_specs, out_specs=out_specs, check_vma=False)
```

```python
from functools import partial

import jax
import jax.numpy as jnp
from jax import lax
from jax.sharding import PartitionSpec as P

HD = 64


epsilon = 1e-06


def shifted(block, axis, distance):
    devices = range(lax.axis_size(axis))
    route = [(i - distance, i) for i in devices if i - distance in devices]
    return lax.ppermute(block, axis, route)


def standardize_rows(values):
    row_means = jnp.mean(values, axis=1, keepdims=True)
    center = values - row_means
    inverse = lax.rsqrt(jnp.mean(center * center, axis=1, keepdims=True) + epsilon)
    return (center * inverse, row_means, inverse)


def contract_rows(left_side, right_side):
    return lax.dot_general(
        left_side, right_side, (((0,), (0,)), ((), ())), preferred_element_type=jnp.float32
    )


def contract_cols(left_side, right_side):
    return lax.dot_general(
        left_side, right_side, (((1,), (1,)), ((), ())), preferred_element_type=jnp.float32
    )


def member_sum(gradients):
    return lax.psum(gradients, "dp")


def tensor_scatter_sum(partial_value):
    group = lax.axis_size("tensor")
    rows_count, full_width = partial_value.shape
    pieces = lax.all_to_all(
        partial_value.astype(jnp.bfloat16), "tensor", 1, 0, tiled=True
    ).reshape(group, rows_count, full_width // group)
    return jnp.sum(pieces.astype(jnp.float32), axis=0)


def tensor_sum(partial_value):
    summed = tensor_scatter_sum(partial_value)
    return lax.all_gather(summed.astype(jnp.bfloat16), "tensor", axis=1, tiled=True).astype(
        jnp.float32
    )


def layer_forward(partial_residual, params, column):
    (
        first_norm_gain,
        first_norm_bias,
        qkv_mat,
        qv_add,
        out_mat,
        out_add,
        second_norm_gain,
        second_norm_bias,
        up_mat,
        up_add,
        down_mat,
        down_add,
    ) = params
    rows_count = partial_residual.shape[0]
    part_width = partial_residual.shape[1]
    hidden_width = first_norm_gain.shape[0]
    head_count = part_width // HD

    complete_residual = lax.all_gather(partial_residual, "tensor", axis=1, tiled=True).astype(
        jnp.float32
    )
    first_centered_unit, first_row_averages, first_inverse_deviation = standardize_rows(
        complete_residual
    )
    first_normalized = (first_centered_unit * first_norm_gain + first_norm_bias).astype(
        jnp.bfloat16
    )
    projected = jnp.dot(
        first_normalized,
        qkv_mat.reshape(hidden_width, 3 * part_width),
        preferred_element_type=jnp.float32,
    ).reshape(rows_count, 3, part_width)
    queries = (projected[:, 0] + qv_add[0]).astype(jnp.bfloat16).reshape(rows_count, head_count, HD)
    keys_part = projected[:, 1].astype(jnp.bfloat16).reshape(rows_count, head_count, HD)
    values_part = (
        (projected[:, 2] + qv_add[1]).astype(jnp.bfloat16).reshape(rows_count, head_count, HD)
    )
    scores = jnp.einsum(
        "qhd,khd->hqk", queries, keys_part, preferred_element_type=jnp.float32
    ) * HD ** (-0.5)
    totals = jax.nn.logsumexp(scores, axis=2, keepdims=True)
    probabilities = jnp.exp(scores - totals)
    attended = (
        jnp.einsum(
            "hqk,khd->qhd",
            probabilities.astype(jnp.bfloat16),
            values_part,
            preferred_element_type=jnp.float32,
        )
        .reshape(rows_count, part_width)
        .astype(jnp.bfloat16)
    )
    branch = tensor_sum(jnp.dot(attended, out_mat, preferred_element_type=jnp.float32))
    middle = complete_residual + branch + out_add
    middle_rounded = middle.astype(jnp.bfloat16).astype(jnp.float32)
    second_centered_unit, second_row_averages, second_inverse_deviation = standardize_rows(
        middle_rounded
    )
    second_normalized = (second_centered_unit * second_norm_gain + second_norm_bias).astype(
        jnp.bfloat16
    )
    hidden_pre = jnp.dot(second_normalized, up_mat, preferred_element_type=jnp.float32) + up_add
    hidden = jax.nn.gelu(hidden_pre, approximate=False).astype(jnp.bfloat16)
    feed_out = tensor_scatter_sum(jnp.dot(hidden, down_mat, preferred_element_type=jnp.float32))
    result_part = (
        lax.dynamic_slice_in_dim(middle, column, part_width, 1)
        + feed_out
        + lax.dynamic_slice_in_dim(down_add, column, part_width, 0)
    )
    saved_state = (
        first_centered_unit,
        first_inverse_deviation,
        first_normalized,
        queries,
        keys_part,
        values_part,
        totals,
        attended,
        second_centered_unit,
        second_inverse_deviation,
        second_normalized,
        hidden_pre,
        hidden,
    )
    return (result_part.astype(jnp.bfloat16), saved_state)


def layer_backward(grad_part, saved_state, params, column, grad_sums):
    (
        first_norm_gain,
        first_norm_bias,
        qkv_mat,
        qv_add,
        out_mat,
        out_add,
        second_norm_gain,
        second_norm_bias,
        up_mat,
        up_add,
        down_mat,
        down_add,
    ) = params
    (
        first_centered_unit,
        first_inverse_deviation,
        first_normalized,
        queries,
        keys_part,
        values_part,
        totals,
        attended,
        second_centered_unit,
        second_inverse_deviation,
        second_normalized,
        hidden_pre,
        hidden,
    ) = saved_state
    rows_count = grad_part.shape[0]
    part_width = grad_part.shape[1]
    hidden_width = first_norm_gain.shape[0]
    head_count = part_width // HD

    def local_cols(matrix):
        return lax.dynamic_slice_in_dim(matrix, column, part_width, 1)

    grad_full_bf16 = lax.all_gather(grad_part, "tensor", axis=1, tiled=True)
    grad_full = grad_full_bf16.astype(jnp.float32)
    down_grad = contract_rows(hidden, grad_full_bf16)
    down_add_grad = jnp.sum(local_cols(grad_full), axis=0)
    hidden_grad = contract_cols(grad_full_bf16, down_mat)
    unused_value, gelu_back = jax.vjp(partial(jax.nn.gelu, approximate=False), hidden_pre)
    pre_grad = gelu_back(hidden_grad)[0].astype(jnp.bfloat16)
    up_grad = contract_rows(second_normalized, pre_grad)
    up_add_grad = jnp.sum(pre_grad.astype(jnp.float32), axis=0)
    normalized_gradient = tensor_sum(contract_cols(pre_grad, up_mat))
    second_gain_gradient = jnp.sum(local_cols(normalized_gradient * second_centered_unit), axis=0)
    bias_two_grad = jnp.sum(local_cols(normalized_gradient), axis=0)
    second_rescaled = normalized_gradient * second_norm_gain
    first_running_total = jnp.sum(second_rescaled, axis=1, keepdims=True)
    second_running_total = jnp.sum(second_rescaled * second_centered_unit, axis=1, keepdims=True)
    middle_grad = grad_full + second_inverse_deviation * (
        second_rescaled
        - first_running_total / hidden_width
        - second_centered_unit * second_running_total / hidden_width
    )
    feed_grads = (
        second_gain_gradient,
        bias_two_grad,
        up_grad,
        up_add_grad,
        down_grad,
        down_add_grad,
    )
    feed_grads = tuple((older + newer for older, newer in zip(grad_sums[6:], feed_grads)))
    branch_grad = middle_grad.astype(jnp.bfloat16)
    out_grad = contract_rows(attended, branch_grad)
    out_add_grad = jnp.sum(local_cols(middle_grad), axis=0)
    attended_grad = (
        contract_cols(branch_grad, out_mat).astype(jnp.bfloat16).reshape(rows_count, head_count, HD)
    )
    scale_factor = HD ** (-0.5)
    scores = (
        jnp.einsum("qhd,khd->hqk", queries, keys_part, preferred_element_type=jnp.float32)
        * scale_factor
    )
    probabilities = jnp.exp(scores - totals)
    values_grad = jnp.einsum(
        "hqk,qhd->khd",
        probabilities.astype(jnp.bfloat16),
        attended_grad,
        preferred_element_type=jnp.float32,
    )
    weight_grad = jnp.einsum(
        "qhd,khd->hqk", attended_grad, values_part, preferred_element_type=jnp.float32
    )
    rowdot = jnp.sum(probabilities * weight_grad, axis=2, keepdims=True)
    score_grad = (probabilities * (weight_grad - rowdot)).astype(jnp.bfloat16)
    query_grad = (
        jnp.einsum("hqk,khd->qhd", score_grad, keys_part, preferred_element_type=jnp.float32)
        * scale_factor
    )
    key_grad = (
        jnp.einsum("hqk,qhd->khd", score_grad, queries, preferred_element_type=jnp.float32)
        * scale_factor
    )
    projected_grad = jnp.stack(
        [
            query_grad.reshape(rows_count, part_width),
            key_grad.reshape(rows_count, part_width),
            values_grad.reshape(rows_count, part_width),
        ],
        axis=1,
    ).astype(jnp.bfloat16)
    flat_grad = projected_grad.reshape(rows_count, 3 * part_width)
    qkv_grad = contract_rows(first_normalized, flat_grad).reshape(hidden_width, 3, part_width)
    qv_add_grad = jnp.stack(
        [
            jnp.sum(projected_grad[:, 0].astype(jnp.float32), axis=0),
            jnp.sum(projected_grad[:, 2].astype(jnp.float32), axis=0),
        ]
    )
    first_normalized_gradient = tensor_sum(
        contract_cols(flat_grad, qkv_mat.reshape(hidden_width, 3 * part_width))
    )
    first_gain_gradient = jnp.sum(
        local_cols(first_normalized_gradient * first_centered_unit), axis=0
    )
    bias_one_grad = jnp.sum(local_cols(first_normalized_gradient), axis=0)
    first_rescaled = first_normalized_gradient * first_norm_gain
    third_running_total = jnp.sum(first_rescaled, axis=1, keepdims=True)
    fourth_running_total = jnp.sum(first_rescaled * first_centered_unit, axis=1, keepdims=True)
    stream_grad = middle_grad + first_inverse_deviation * (
        first_rescaled
        - third_running_total / hidden_width
        - first_centered_unit * fourth_running_total / hidden_width
    )
    attention_grads = (
        first_gain_gradient,
        bias_one_grad,
        qkv_grad,
        qv_add_grad,
        out_grad,
        out_add_grad,
    )
    attention_grads = tuple((older + newer for older, newer in zip(grad_sums[:6], attention_grads)))
    return (local_cols(stream_grad), attention_grads + feed_grads)


def swap_sections(value):
    return lax.ppermute(value, "section", [(0, 1), (1, 0)])


def pack_small(grads):
    (g1, b1, qkv, qv, out, ob, g2, b2, fc1, fc1b, fc2, fc2b) = grads
    rows = jnp.stack(
        [
            jnp.concatenate([g1, b1, qv[0], qv[1]]),
            jnp.concatenate([ob, g2, b2, fc2b]),
            fc1b,
        ]
    )
    return (qkv, out, fc1, jnp.concatenate([fc2, rows], axis=0))


def unpack_small(packed, part_width):
    qkv, out, fc1, fc2_ext = packed
    fc2 = fc2_ext[:-3]
    rows = fc2_ext[-3:]
    w = part_width

    def piece(row, index):
        return rows[row, index * w : (index + 1) * w]

    qv = jnp.stack([piece(0, 2), piece(0, 3)])
    return (
        piece(0, 0),
        piece(0, 1),
        qkv,
        qv,
        out,
        piece(1, 0),
        piece(1, 1),
        piece(1, 2),
        fc1,
        rows[2],
        fc2,
        piece(1, 3),
    )


def shards(
    images,
    slot_table,
    ln1_gain,
    ln1_bias,
    qkv_weight,
    qv_bias,
    out_weight,
    out_bias,
    ln2_gain,
    ln2_bias,
    fc1_weight,
    fc1_bias,
    fc2_weight,
    fc2_bias,
    cotangent,
):
    own_params = tuple(
        (
            weight_arg[0]
            for weight_arg in (
                ln1_gain,
                ln1_bias,
                qkv_weight,
                qv_bias,
                out_weight,
                out_bias,
                ln2_gain,
                ln2_bias,
                fc1_weight,
                fc1_bias,
                fc2_weight,
                fc2_bias,
            )
        )
    )
    other_params = tuple(swap_sections(weight) for weight in own_params)
    section_index = lax.axis_index("section")
    first_section = section_index == 0
    first_params = tuple(
        jnp.where(first_section, mine, theirs) for mine, theirs in zip(own_params, other_params)
    )
    second_params = tuple(
        jnp.where(first_section, theirs, mine) for mine, theirs in zip(own_params, other_params)
    )
    part_width = images.shape[2]
    column = lax.axis_index("tensor") * part_width
    slot_count = images.shape[0]
    slot_ids = jnp.arange(slot_count, dtype=jnp.int32)

    mine_slot = lax.dynamic_index_in_dim(slot_table, section_index, 0, keepdims=False)
    theirs_slot = lax.dynamic_index_in_dim(slot_table, 1 - section_index, 0, keepdims=False)
    mine_active = mine_slot < slot_count
    theirs_active = theirs_slot < slot_count
    mine_placed = (slot_ids == mine_slot) & mine_active
    theirs_placed = (slot_ids == theirs_slot) & theirs_active
    where_from = jnp.minimum(mine_slot, slot_count - 1)

    own_image = lax.dynamic_index_in_dim(images, where_from, 0, keepdims=False)
    first_out, first_state = layer_forward(own_image, first_params, column)
    second_out, second_state = layer_forward(first_out, second_params, column)
    kept_out = jnp.where(first_section, first_out, second_out)
    sent_out = swap_sections(jnp.where(first_section, second_out, first_out))
    layer_outputs = (
        mine_placed[:, None, None].astype(jnp.bfloat16) * kept_out[None]
        + theirs_placed[:, None, None].astype(jnp.bfloat16) * sent_out[None]
    )

    def zeros_of(extent):
        return jnp.zeros(extent, jnp.float32)

    empty_sums = (
        zeros_of((part_width,)),
        zeros_of((part_width,)),
        zeros_of(own_params[2].shape),
        zeros_of(own_params[3].shape),
        zeros_of(own_params[4].shape),
        zeros_of((part_width,)),
        zeros_of((part_width,)),
        zeros_of((part_width,)),
        zeros_of(own_params[8].shape),
        zeros_of(own_params[9].shape),
        zeros_of(own_params[10].shape),
        zeros_of((part_width,)),
    )
    own_grad = lax.dynamic_index_in_dim(cotangent, where_from, 0, keepdims=False)
    entering = jnp.where(mine_active, own_grad, jnp.zeros_like(own_grad))
    second_dz, second_grads = layer_backward(
        entering, second_state, second_params, column, empty_sums
    )
    second_sums = lax.psum(pack_small(second_grads), ("section", "dp"))
    first_dz, first_grads = layer_backward(
        second_dz.astype(jnp.bfloat16), first_state, first_params, column, empty_sums
    )
    first_packed, second_sums = lax.optimization_barrier((pack_small(first_grads), second_sums))
    first_sums = lax.psum(first_packed, ("section", "dp"))
    kept_dz = jnp.where(first_section, first_dz, second_dz)
    sent_dz = swap_sections(jnp.where(first_section, second_dz, first_dz))
    grads_in = (
        mine_placed[:, None, None].astype(jnp.float32) * kept_dz[None]
        + theirs_placed[:, None, None].astype(jnp.float32) * sent_dz[None]
    )
    grad_sums = unpack_small(
        tuple(
            jnp.where(first_section, early, late) for early, late in zip(first_sums, second_sums)
        ),
        part_width,
    )
    return (layer_outputs[None], grads_in[None]) + tuple((gradient[None] for gradient in grad_sums))


def solution(mesh):
    in_specs = (
        P("dp", None, "tensor"),
        P("dp"),
        P("section", None),
        P("section", None),
        P("section", None, None, "tensor"),
        P("section", None, "tensor"),
        P("section", "tensor", None),
        P("section", None),
        P("section", None),
        P("section", None),
        P("section", None, "tensor"),
        P("section", "tensor"),
        P("section", "tensor", None),
        P("section", None),
        P("dp", None, "tensor"),
    )
    out_specs = (
        P("section", "dp", None, "tensor"),
        P("section", "dp", None, "tensor"),
        P("section", "tensor"),
        P("section", "tensor"),
        P("section", None, None, "tensor"),
        P("section", None, "tensor"),
        P("section", "tensor", None),
        P("section", "tensor"),
        P("section", "tensor"),
        P("section", "tensor"),
        P("section", None, "tensor"),
        P("section", "tensor"),
        P("section", "tensor", None),
        P("section", "tensor"),
    )
    return jax.shard_map(shards, mesh=mesh, in_specs=in_specs, out_specs=out_specs, check_vma=False)
```
